32 devices in a mesh: groups: 2 (over y), space: 4 (over z), wave: 4 (over x, core).
Axes of the slice: x: 2, y: 2, z: 4, core: 2. Of those that a mesh axis runs over, the one named last changes fastest.
Arguments:
- density: float32 [512, 16, 128], P(('groups', 'space')), parts along dimension 0, may hold values from -6 to 6
- even_taps: float32 [15], replicated, may hold values from -1.5 to 1.5
- odd_taps: float32 [15], replicated, may hold values from -1.5 to 1.5
- low_taps: float32 [15], replicated, may hold values from -1.5 to 1.5
- wavelets: int32 [40, 2], replicated, may hold values from 0 to 2, as said below
- pairs: int32 [32, 2], replicated, may hold values from -1 to 39, as said below
Outputs:
- second: float32 [32, 256, 8, 64], P('wave', ('groups', 'space')), parts along dimension 1
The draws below stay inside these ranges and needn't reach their ends.
There are 2 independent parts, one for each index of `groups`. The reference program is written for one: setup_inputs(seed, part) draws one part's arguments, and reference() takes and returns one part's arrays. A program takes and returns all parts, laid end to end along the dimension named above; an argument that names none is the same for every part. Nothing has to cross between parts.
Inputs may be any that keep to these rules, and one draw needn't show every extreme that they name: `wavelets`: column 0 is a dilation level below 3, column 1 an orientation 0, 1 or 2. Rows below 5 have levels below 2; the last row has level 2. `pairs`: the slots form aligned blocks of 8 rows, one block for each index of wave. In every block the live rows come first and at least one is live; some block has all 8 rows live. A live row holds a first-order field below 5 and a wavelet row of 5 or more whose level is above that field's level; a dead row is (-1, 0).
All inputs are finite; a program needn't handle non-finite values.
Results may differ from the reference program's by a relative error of at most 0.0003.
Values sent between devices are 32-bit elements; how exact they have to be, the bound alone decides.
A program may use at most 64 MiB of HBM per device.

```python
import jax
import jax.numpy as jnp
from jax import lax

NY = 16
NZ = 128
PAIR_DEV = 8
NFIRST = 5
NWAVE = 40
TAPS = 15
LEVELS = 3
REACH = 28
NX = 256
PAIRS = 32


def wavelet_table(key):
    first_levels = jax.random.randint(jax.random.fold_in(key, 11), (NWAVE,), 0, LEVELS - 1)
    other_levels = jax.random.randint(jax.random.fold_in(key, 16), (NWAVE,), 0, LEVELS)
    rows = jnp.arange(NWAVE)
    level_draw = jnp.where(rows < NFIRST, first_levels, other_levels)
    orient_draw = jax.random.randint(jax.random.fold_in(key, 12), (NWAVE,), 0, 3)
    level_draw = level_draw.at[NWAVE - 1].set(LEVELS - 1)
    orient_draw = orient_draw.at[0].set(2)
    return jnp.stack([level_draw, orient_draw], axis=1).astype(jnp.int32)


def draw_wavelets(key, part):
    return wavelet_table(key)


def draw_pairs(key, part):
    table = wavelet_table(key)
    levels = table[:, 0]
    block_count = PAIRS // PAIR_DEV
    ranking = jax.random.permutation(jax.random.fold_in(key, 13), block_count)
    heights = ranking + 1
    squared = block_count * block_count
    live_counts = jnp.maximum(1, (PAIR_DEV * heights * heights + squared - 1) // squared)
    positions = jnp.arange(PAIRS)
    slot_in_block = positions % PAIR_DEV
    block_of = positions // PAIR_DEV
    live_flags = slot_in_block < live_counts[block_of]
    field_draw = jax.random.randint(jax.random.fold_in(key, 14), (PAIRS,), 0, NFIRST)
    field_levels = levels[field_draw]
    rows = jnp.arange(NWAVE)
    eligible = (rows[None, :] >= NFIRST) & (levels[None, :] > field_levels[:, None])
    scores = jax.random.randint(jax.random.fold_in(key, 15), (PAIRS, NWAVE), 0, 1 << 20) * 64 + rows[None, :]
    scores = jnp.where(eligible, scores, -1)
    wave_draw = jnp.argmax(scores, axis=1).astype(jnp.int32)
    busiest = (ranking[block_of] == block_count - 1) & (slot_in_block == 0)
    wave_draw = jnp.where(busiest, NWAVE - 1, wave_draw)
    first_col = jnp.where(live_flags, field_draw, -1)
    second_col = jnp.where(live_flags, wave_draw, 0)
    return jnp.stack([first_col, second_col], axis=1).astype(jnp.int32)


def block_scale(key, shape, pieces, low, high):
    gain = 1.0
    for dim, shards_of in pieces:
        steps = jax.random.uniform(jax.random.fold_in(jax.random.fold_in(key, 6), dim), (shards_of,), jnp.float32, low / len(pieces), high / len(pieces))
        gain = gain * jnp.repeat(jnp.exp(steps), shape[dim] // shards_of).reshape((-1,) + (1,) * (len(shape) - 1 - dim))
    return gain


def centred(key, shape, scale, reach, shards=(), kind=jnp.bfloat16):
    result = scale * jax.random.normal(key, shape, jnp.float32)
    if shards:
        result = result * block_scale(key, shape, shards, -0.22, 0.18)
    return jnp.clip(result, -reach, reach).astype(kind)


def setup_inputs(seed: int = 0, part: int = 0) -> dict:
    key_of = jax.random.split(jax.random.key(seed), 7)
    own_keys = jax.random.split(jax.random.fold_in(key_of[6], part), 7)
    density = centred(own_keys[0], (NX, NY, NZ), 1.0, 6.0, ((0, 4),), jnp.float32)
    even_taps = centred(key_of[1], (TAPS,), TAPS ** -0.5, 1.5, (), jnp.float32)
    odd_taps = centred(key_of[2], (TAPS,), TAPS ** -0.5, 1.5, (), jnp.float32)
    low_taps = centred(key_of[3], (TAPS,), TAPS ** -0.5, 1.5, (), jnp.float32)
    wavelets = draw_wavelets(jax.random.fold_in(key_of[6], 71), part)
    pairs = draw_pairs(jax.random.fold_in(key_of[6], 71), part)
    return {"density": density, "even_taps": even_taps, "odd_taps": odd_taps, "low_taps": low_taps, "wavelets": wavelets, "pairs": pairs}


def widen(values_in, direction, margin):
    widths = [(0, 0)] * values_in.ndim
    widths[direction] = (margin, margin)
    return jnp.pad(values_in, widths)

def along(values_in, weights, dilation, direction, length_out):
    centre = weights.shape[0] // 2
    accumulated = None
    for tap_index in range(weights.shape[0]):
        offset = REACH + (tap_index - centre) * dilation
        shifted = lax.dynamic_slice_in_dim(values_in, offset, length_out, direction)
        weighted = weights[tap_index] * shifted
        accumulated = weighted if accumulated is None else accumulated + weighted
    return accumulated

def respond(values_in, level_index, orient, filters, length_out):
    even_taps, odd_taps, low_taps = filters
    dilation = jnp.left_shift(jnp.int32(1), level_index.astype(jnp.int32))

    def make_branch(band):

        def respond_oriented(source):
            signals = (source,)
            for direction in range(3):
                if direction == 0:
                    extent = length_out
                    prepared = signals
                else:
                    extent = source.shape[direction]
                    prepared = tuple((widen(signal, direction, REACH) for signal in signals))
                if direction == band:
                    signals = (along(prepared[0], even_taps, dilation, direction, extent), along(prepared[0], odd_taps, dilation, direction, extent))
                else:
                    signals = tuple((along(signal, low_taps, dilation, direction, extent) for signal in prepared))
            real_part, imag_part = signals
            return jnp.sqrt(real_part * real_part + imag_part * imag_part + 1e-06)
        return respond_oriented
    return lax.switch(orient.astype(jnp.int32), [make_branch(0), make_branch(1), make_branch(2)], values_in)

def reference(density, even_taps, odd_taps, low_taps, wavelets, pairs):
    filters = (even_taps, odd_taps, low_taps)
    wide_density = widen(density, 0, REACH)
    firsts = jnp.stack([respond(wide_density, wavelets[field_index, 0], wavelets[field_index, 1], filters, NX) for field_index in range(NFIRST)])
    first_wide = widen(firsts, 1, REACH)

    def one_pair(pair_row):
        source = lax.dynamic_index_in_dim(first_wide, jnp.maximum(pair_row[0], 0), 0, keepdims=False)

        def work_pair(values_in):
            level_index = wavelets[pair_row[1], 0]
            orient = wavelets[pair_row[1], 1]
            return respond(values_in, level_index, orient, filters, NX)[::2, ::2, ::2]

        def skip_pair(values_in):
            return jnp.zeros((NX // 2, NY // 2, NZ // 2), values_in.dtype)
        return lax.cond(pair_row[0] >= 0, work_pair, skip_pair, source)
    return lax.map(one_pair, pairs)
```

```python
import functools

import jax
import jax.numpy as jnp
from jax import lax
from jax.experimental import pallas as pl
from jax.experimental.pallas import tpu as pltpu
from jax.sharding import PartitionSpec as P

NFIRST = 5
REACH1 = 14
REACH2 = 28
HALO = REACH1 + REACH2
GROUP = 8
BF = jnp.bfloat16


def split_outside(t):
    hi = lax.reduce_precision(t, 8, 7)
    return hi.astype(BF), (t - hi).astype(BF)


def band(diff, taps, dilation):
    count = taps.shape[0]
    total = jnp.zeros(diff.shape, jnp.float32)
    for t in range(count):
        total = jnp.where(diff == (t - count // 2) * dilation, taps[t], total)
    return total


def tables(filters, ny, nz):
    def zdiff(n_out, stride):
        i = lax.broadcasted_iota(jnp.int32, (nz, n_out), 0)
        j = lax.broadcasted_iota(jnp.int32, (nz, n_out), 1)
        return i - j * stride

    def ytable(taps, d, stride):
        n_out = ny // stride
        r = lax.broadcasted_iota(jnp.int32, (GROUP * n_out, GROUP * ny), 0)
        c = lax.broadcasted_iota(jnp.int32, (GROUP * n_out, GROUP * ny), 1)
        t = band(c % ny - (r % n_out) * stride, taps, d)
        hi, lo = split_outside(jnp.where(r // n_out == c // ny, t, 0.0))
        return jnp.concatenate([hi, hi, lo], axis=1)

    z1, y1, z2, y2 = [], [], [], []
    for level in (0, 1):
        for taps in filters:
            hi, lo = split_outside(band(zdiff(nz, 1), taps, 1 << level))
            z1.append(
                jnp.concatenate(
                    [
                        jnp.concatenate([hi, lo], axis=1),
                        jnp.concatenate([hi, jnp.zeros_like(lo)], axis=1),
                    ],
                    axis=0,
                )
            )
            y1.append(ytable(taps, 1 << level, 1))
    for level in (1, 2):
        parts = [split_outside(band(zdiff(nz // 2, 2), taps, 1 << level)) for taps in filters]
        zero = jnp.zeros((nz, nz // 2), BF)
        none = (zero, zero)
        for left, right in ((parts[2], none), (none, parts[2]), (parts[0], parts[1])):
            z2.append(
                jnp.concatenate(
                    [
                        jnp.concatenate([left[0], right[0], left[1], right[1]], axis=1),
                        jnp.concatenate([left[0], right[0], zero, zero], axis=1),
                    ],
                    axis=0,
                )
            )
        for taps in filters:
            y2.append(ytable(taps, 1 << level, 2))
    return jnp.stack(z1), jnp.stack(y1), jnp.stack(z2), jnp.stack(y2)


def halves(v):
    hi = v.astype(BF)
    return hi, (v - hi.astype(jnp.float32)).astype(BF)


def stacked(v):
    hi, lo = halves(v)
    return jnp.concatenate([hi, lo, hi], axis=0)


def beside(v):
    hi, lo = halves(v)
    return jnp.concatenate([hi, lo], axis=1)


def dot(a, b):
    return jnp.dot(a, b, preferred_element_type=jnp.float32)


def folded(r):
    n = r.shape[1] // 2
    return r[:, :n] + r[:, n:]


def xpass(load, tap_sets):
    count = tap_sets[0].shape[0]
    accs = [[None] * GROUP for _ in tap_sets]
    for t in range(count):
        weights = [s[t] for s in tap_sets]
        for k in range(GROUP):
            plane = load(t, k)
            for n, w in enumerate(weights):
                term = w * plane
                accs[n][k] = term if t == 0 else accs[n][k] + term
    return [jnp.concatenate(a, axis=0) for a in accs]


def kernel(
    rows,
    wav,
    pairs,
    even,
    odd,
    low,
    before,
    centre,
    after,
    z1,
    y1,
    z2,
    y2,
    out,
    ext,
    firsts,
    sems,
):
    ny, nz = ext.shape[1], ext.shape[2]
    per_dev = out.shape[0]
    taps_half = even.shape[0] // 2
    fields = rows + 2 * REACH2
    copies = [
        pltpu.make_async_copy(before, ext.at[pl.ds(0, HALO)], sems.at[0]),
        pltpu.make_async_copy(centre, ext.at[pl.ds(HALO, rows)], sems.at[1]),
        pltpu.make_async_copy(after, ext.at[pl.ds(HALO + rows, HALO)], sems.at[2]),
    ]
    for copy in copies:
        copy.start()
    for copy in copies:
        copy.wait()
    space = lax.axis_index("space")
    start = lax.axis_index("wave") * per_dev

    def first_steps(f, orient, unroll):
        level = wav[f, 0]
        d = jnp.left_shift(jnp.int32(1), level)
        tab = level * 3

        def step(i, carry):
            chains = []
            for u in range(unroll):
                base = (i * unroll + u) * GROUP + REACH1

                def load(t, k):
                    return ext[base + k + (t - taps_half) * d]

                xs = xpass(load, (even, odd) if orient == 0 else (low,))
                if orient == 1:
                    src = stacked(xs[0])
                    ys = [dot(y1[tab], src), dot(y1[tab + 1], src)]
                else:
                    ys = [dot(y1[tab + 2], stacked(x)) for x in xs]
                chains.append(ys)
            cols = [beside(jnp.concatenate(c, axis=0)) for c in zip(*chains)]
            if orient == 2:
                re = folded(dot(cols[0], z1[tab]))
                im = folded(dot(cols[0], z1[tab + 1]))
            else:
                re = folded(dot(cols[0], z1[tab + 2]))
                im = folded(dot(cols[1], z1[tab + 2]))
            mag = jnp.sqrt(re * re + im * im + 1e-06)
            planes = unroll * GROUP
            firsts[f, pl.ds(i * planes, planes)] = mag.reshape(planes, ny, nz)
            return carry

        lax.fori_loop(0, fields // (unroll * GROUP), step, 0)

    def do_first(f, carry):
        need = jnp.int32(0)
        for p in range(per_dev):
            need = need + (pairs[start + p, 0] == f).astype(jnp.int32)
        for orient in range(3):

            @pl.when((need > 0) & (wav[f, 1] == orient))
            def _():
                first_steps(f, orient, 3 if fields % (3 * GROUP) == 0 else 1)

        @pl.when(space == 0)
        def _():
            firsts[f, pl.ds(0, REACH2)] = jnp.zeros((REACH2, ny, nz), jnp.float32)

        @pl.when(space == lax.axis_size("space") - 1)
        def _():
            firsts[f, pl.ds(REACH2 + rows, REACH2)] = jnp.zeros((REACH2, ny, nz), jnp.float32)

        return carry

    lax.fori_loop(0, NFIRST, do_first, 0)

    def second_steps(p, f, w, orient):
        level = wav[w, 0]
        d = jnp.left_shift(jnp.int32(1), level)
        tab = (level - 1) * 3
        chains = []
        for g in range(rows // 2 // GROUP):

            def load(t, k):
                return firsts[f, REACH2 + 2 * (g * GROUP + k) + (t - taps_half) * d]

            xs = xpass(load, (even, odd) if orient == 0 else (low,))
            if orient == 1:
                src = stacked(xs[0])
                ys = [dot(y2[tab], src), dot(y2[tab + 1], src)]
            else:
                ys = [dot(y2[tab + 2], stacked(x)) for x in xs]
            chains.append(ys)
        cols = [beside(jnp.concatenate(c, axis=0)) for c in zip(*chains)]
        if orient == 2:
            r = dot(cols[0], z2[tab + 2])
        else:
            r = dot(cols[0], z2[tab]) + dot(cols[1], z2[tab + 1])
        v = folded(r)
        sq = v * v
        total = sq + pltpu.roll(sq, nz // 2, 1)
        mag = jnp.sqrt(total + 1e-06)[:, : nz // 2]
        out[p] = mag.reshape(out.shape[1:])

    def do_pair(p, carry):
        f = pairs[start + p, 0]
        w = pairs[start + p, 1]
        for orient in range(3):

            @pl.when((f >= 0) & (wav[w, 1] == orient))
            def _():
                second_steps(p, f, w, orient)

        @pl.when(f < 0)
        def _():
            out[p] = jnp.zeros(out.shape[1:], jnp.float32)

        return carry

    lax.fori_loop(0, per_dev, do_pair, 0)


def shards(density, even_taps, odd_taps, low_taps, wavelets, pairs):
    rows, ny, nz = density.shape
    count = lax.axis_size("space")
    up = [(i, i + 1) for i in range(count - 1)]
    down = [(j, i) for i, j in up]
    before = lax.ppermute(density[rows - HALO :], "space", up)
    after = lax.ppermute(density[:HALO], "space", down)
    z1, y1, z2, y2 = tables((even_taps, odd_taps, low_taps), ny, nz)
    per_dev = pairs.shape[0] // lax.axis_size("wave")
    smem = pl.BlockSpec(memory_space=pltpu.SMEM)
    vmem = pl.BlockSpec(memory_space=pltpu.VMEM)
    anyw = pl.BlockSpec(memory_space=pl.ANY)
    return pl.pallas_call(
        functools.partial(kernel, rows),
        out_shape=jax.ShapeDtypeStruct((per_dev, rows // 2, ny // 2, nz // 2), jnp.float32),
        in_specs=[smem] * 5 + [anyw] * 3 + [vmem] * 4,
        out_specs=vmem,
        scratch_shapes=[
            pltpu.VMEM((rows + 2 * HALO, ny, nz), jnp.float32),
            pltpu.VMEM((NFIRST, rows + 2 * REACH2, ny, nz), jnp.float32),
            pltpu.SemaphoreType.DMA((3,)),
        ],
        name="scatter",
    )(wavelets, pairs, even_taps, odd_taps, low_taps, before, density, after, z1, y1, z2, y2)


def solution(mesh):
    placed = (P(("groups", "space"), None, None), P(), P(), P(), P(), P())
    return jax.shard_map(
        shards,
        mesh=mesh,
        in_specs=placed,
        out_specs=P("wave", ("groups", "space"), None, None),
        check_vma=False,
    )
```

```python
import functools

import jax
import jax.numpy as jnp
from jax import lax
from jax.experimental import pallas as pl
from jax.experimental.pallas import tpu as pltpu
from jax.sharding import PartitionSpec as P

NFIRST = 5
REACH1 = 14
REACH2 = 28
HALO = REACH1 + REACH2
GROUP = 8
CHUNKS = 3
BF = jnp.bfloat16


def halves(v):
    hi = v.astype(BF)
    return hi, (v - hi.astype(jnp.float32)).astype(BF)


def band(diff, tap_sets, dilation, extent):
    count = tap_sets[0].shape[0]
    totals = [jnp.zeros(diff.shape, jnp.float32) for _ in tap_sets]
    for t in range(count):
        offset = (t - count // 2) * dilation
        if abs(offset) < extent:
            hit = diff == offset
            totals = [jnp.where(hit, s[t], v) for s, v in zip(tap_sets, totals)]
    return totals


def build_tables(filters, ny, nz, z1, y1, z2, y2):
    even, odd, low = filters
    blk = 32

    def iotas(r0, shape):
        r = lax.broadcasted_iota(jnp.int32, shape, 0) + r0
        return r, lax.broadcasted_iota(jnp.int32, shape, 1)

    def put_z(ref, n, r0, value):
        hi, lo = halves(value)
        ref[n, pl.ds(r0, blk), pl.ds(0, nz)] = hi
        ref[n, pl.ds(r0, blk), pl.ds(nz, nz)] = lo
        ref[n, pl.ds(nz + r0, blk), pl.ds(0, nz)] = hi
        ref[n, pl.ds(nz + r0, blk), pl.ds(nz, nz)] = jnp.zeros_like(lo)

    def put_y(ref, n, r0, value):
        hi, lo = halves(value)
        width = GROUP * ny
        ref[n, pl.ds(r0, blk), pl.ds(0, width)] = hi
        ref[n, pl.ds(r0, blk), pl.ds(width, width)] = hi
        ref[n, pl.ds(r0, blk), pl.ds(2 * width, width)] = lo

    for level in (0, 1):
        for r0 in range(0, nz, blk):
            i, j = iotas(r0, (blk, nz))
            for n, v in enumerate(band(i - j, filters, 1 << level, nz)):
                put_z(z1, level * 3 + n, r0, v)
    for stride, ref, levels in ((1, y1, (0, 1)), (2, y2, (1, 2))):
        n_out = ny // stride
        for r0 in range(0, GROUP * n_out, blk):
            r, c = iotas(r0, (blk, GROUP * ny))
            diff = jnp.where(r // n_out == c // ny, c % ny - (r % n_out) * stride, 4 * ny)
            for at, level in enumerate(levels):
                for n, v in enumerate(band(diff, filters, 1 << level, ny)):
                    put_y(ref, at * 3 + n, r0, v)
    half = nz // 2
    for at, level in enumerate((1, 2)):
        for r0 in range(0, nz, blk):
            i, j = iotas(r0, (blk, nz))
            left = j < half
            diff = i - 2 * jnp.where(left, j, j - half)
            e, o, l = band(diff, filters, 1 << level, nz)
            put_z(z2, at * 3, r0, jnp.where(left, l, 0.0))
            put_z(z2, at * 3 + 1, r0, jnp.where(left, 0.0, l))
            put_z(z2, at * 3 + 2, r0, jnp.where(left, e, o))


def exchange(even, odd, low, density, before, after, z1, y1, z2, y2, zsend, zrecv, psend, precv):
    rows, ny, nz = density.shape
    chunk = HALO // 2 // CHUNKS
    count = lax.axis_size("space")
    space = lax.axis_index("space")
    wave = lax.axis_index("wave")
    core = lax.rem(wave, 2)
    partner = wave + 1 - 2 * core
    above = space < count - 1
    below = space > 0
    mesh_ids = pl.DeviceIdType.MESH
    barrier = pltpu.get_barrier_semaphore()

    @pl.when(above)
    def _():
        pl.semaphore_signal(barrier, 1, device_id={"space": space + 1}, device_id_type=mesh_ids)

    @pl.when(below)
    def _():
        pl.semaphore_signal(barrier, 1, device_id={"space": space - 1}, device_id_type=mesh_ids)

    pl.semaphore_signal(barrier, 1, device_id={"wave": partner}, device_id_type=mesh_ids)
    peers = 1 + above.astype(jnp.int32) + below.astype(jnp.int32)
    pl.semaphore_wait(barrier, peers)

    landing = (before, after)
    sends = (above, below)
    arrives = (below, above)

    def zcopy(way, q):
        r = core * (HALO // 2) + q * chunk
        return pltpu.make_async_remote_copy(
            src_ref=density.at[pl.ds(r + (rows - HALO if way == 0 else 0), chunk)],
            dst_ref=landing[way].at[pl.ds(r, chunk)],
            send_sem=zsend.at[way, q],
            recv_sem=zrecv.at[way, q],
            device_id={"space": space + 1 if way == 0 else space - 1},
            device_id_type=mesh_ids,
        )

    def pcopy(way, q, first):
        part = landing[way].at[pl.ds(first * (HALO // 2) + q * chunk, chunk)]
        return pltpu.make_async_remote_copy(
            src_ref=part,
            dst_ref=part,
            send_sem=psend.at[way, q],
            recv_sem=precv.at[way, q],
            device_id={"wave": partner},
            device_id_type=mesh_ids,
        )

    every = [(way, q) for q in range(CHUNKS) for way in range(2)]
    for way, q in every:

        @pl.when(sends[way])
        def _():
            zcopy(way, q).start()

    build_tables((even, odd, low), ny, nz, z1, y1, z2, y2)
    for way, q in every:

        @pl.when(arrives[way])
        def _():
            zcopy(way, q).wait_recv()
            pcopy(way, q, core).start()

    for way, q in every:

        @pl.when(sends[way])
        def _():
            zcopy(way, q).wait_send()

        @pl.when(arrives[way])
        def _():
            pcopy(way, q, core).wait_send()
            pcopy(way, q, 1 - core).wait_recv()


def stacked(v):
    hi, lo = halves(v)
    return jnp.concatenate([hi, lo, hi], axis=0)


def beside(v):
    hi, lo = halves(v)
    return jnp.concatenate([hi, lo], axis=1)


def dot(a, b):
    return jnp.dot(a, b, preferred_element_type=jnp.float32)


def folded(r):
    n = r.shape[1] // 2
    return r[:, :n] + r[:, n:]


def xpass(load, tap_sets):
    count = tap_sets[0].shape[0]
    accs = [[None] * GROUP for _ in tap_sets]
    for t in range(count):
        weights = [s[t] for s in tap_sets]
        for k in range(GROUP):
            plane = load(t, k)
            for n, w in enumerate(weights):
                term = w * plane
                accs[n][k] = term if t == 0 else accs[n][k] + term
    return [jnp.concatenate(a, axis=0) for a in accs]


def kernel(
    rows,
    wav,
    pairs,
    even,
    odd,
    low,
    before,
    centre,
    after,
    z1,
    y1,
    z2,
    y2,
    out,
    ext,
    firsts,
    sems,
):
    ny, nz = ext.shape[1], ext.shape[2]
    per_dev = out.shape[0]
    taps_half = even.shape[0] // 2
    fields = rows + 2 * REACH2
    space = lax.axis_index("space")
    last = lax.axis_size("space") - 1
    inner = pltpu.make_async_copy(centre, ext.at[pl.ds(HALO, rows)], sems.at[1])
    inner.start()
    edges = (
        (space > 0, pltpu.make_async_copy(before, ext.at[pl.ds(0, HALO)], sems.at[0]), 0),
        (
            space < last,
            pltpu.make_async_copy(after, ext.at[pl.ds(HALO + rows, HALO)], sems.at[2]),
            HALO + rows,
        ),
    )
    for there, copy, at in edges:

        @pl.when(there)
        def _():
            copy.start()

        @pl.when(jnp.logical_not(there))
        def _():
            ext[pl.ds(at, HALO)] = jnp.zeros((HALO, ny, nz), jnp.float32)

    for there, copy, _ in edges:

        @pl.when(there)
        def _():
            copy.wait()

    inner.wait()
    start = lax.axis_index("wave") * per_dev

    def first_steps(f, orient, unroll):
        level = wav[f, 0]
        d = jnp.left_shift(jnp.int32(1), level)
        tab = level * 3

        def step(i, carry):
            chains = []
            for u in range(unroll):
                base = (i * unroll + u) * GROUP + REACH1

                def load(t, k):
                    return ext[base + k + (t - taps_half) * d]

                xs = xpass(load, (even, odd) if orient == 0 else (low,))
                if orient == 1:
                    src = stacked(xs[0])
                    ys = [dot(y1[tab], src), dot(y1[tab + 1], src)]
                else:
                    ys = [dot(y1[tab + 2], stacked(x)) for x in xs]
                chains.append(ys)
            cols = [beside(jnp.concatenate(c, axis=0)) for c in zip(*chains)]
            if orient == 2:
                re = folded(dot(cols[0], z1[tab]))
                im = folded(dot(cols[0], z1[tab + 1]))
            else:
                re = folded(dot(cols[0], z1[tab + 2]))
                im = folded(dot(cols[1], z1[tab + 2]))
            mag = jnp.sqrt(re * re + im * im + 1e-06)
            planes = unroll * GROUP
            firsts[f, pl.ds(i * planes, planes)] = mag.reshape(planes, ny, nz)
            return carry

        lax.fori_loop(0, fields // (unroll * GROUP), step, 0)

    def do_first(f, carry):
        need = jnp.int32(0)
        for p in range(per_dev):
            need = need + (pairs[start + p, 0] == f).astype(jnp.int32)
        for orient in range(3):

            @pl.when((need > 0) & (wav[f, 1] == orient))
            def _():
                first_steps(f, orient, 3 if fields % (3 * GROUP) == 0 else 1)

        @pl.when(space == 0)
        def _():
            firsts[f, pl.ds(0, REACH2)] = jnp.zeros((REACH2, ny, nz), jnp.float32)

        @pl.when(space == last)
        def _():
            firsts[f, pl.ds(REACH2 + rows, REACH2)] = jnp.zeros((REACH2, ny, nz), jnp.float32)

        return carry

    lax.fori_loop(0, NFIRST, do_first, 0)

    def second_steps(p, f, w, orient):
        level = wav[w, 0]
        d = jnp.left_shift(jnp.int32(1), level)
        tab = (level - 1) * 3
        chains = []
        for g in range(rows // 2 // GROUP):

            def load(t, k):
                return firsts[f, REACH2 + 2 * (g * GROUP + k) + (t - taps_half) * d]

            xs = xpass(load, (even, odd) if orient == 0 else (low,))
            if orient == 1:
                src = stacked(xs[0])
                ys = [dot(y2[tab], src), dot(y2[tab + 1], src)]
            else:
                ys = [dot(y2[tab + 2], stacked(x)) for x in xs]
            chains.append(ys)
        cols = [beside(jnp.concatenate(c, axis=0)) for c in zip(*chains)]
        if orient == 2:
            r = dot(cols[0], z2[tab + 2])
        else:
            r = dot(cols[0], z2[tab]) + dot(cols[1], z2[tab + 1])
        v = folded(r)
        sq = v * v
        total = sq + pltpu.roll(sq, nz // 2, 1)
        mag = jnp.sqrt(total + 1e-06)[:, : nz // 2]
        out[p] = mag.reshape(out.shape[1:])

    def do_pair(p, carry):
        f = pairs[start + p, 0]
        w = pairs[start + p, 1]
        for orient in range(3):

            @pl.when((f >= 0) & (wav[w, 1] == orient))
            def _():
                second_steps(p, f, w, orient)

        @pl.when(f < 0)
        def _():
            out[p] = jnp.zeros(out.shape[1:], jnp.float32)

        return carry

    lax.fori_loop(0, per_dev, do_pair, 0)


def shards(density, even_taps, odd_taps, low_taps, wavelets, pairs):
    rows, ny, nz = density.shape
    per_dev = pairs.shape[0] // lax.axis_size("wave")
    smem = pl.BlockSpec(memory_space=pltpu.SMEM)
    vmem = pl.BlockSpec(memory_space=pltpu.VMEM)
    anyw = pl.BlockSpec(memory_space=pl.ANY)
    halo = jax.ShapeDtypeStruct((HALO, ny, nz), jnp.float32)
    before, after, z1, y1, z2, y2 = pl.pallas_call(
        exchange,
        out_shape=(
            halo,
            halo,
            jax.ShapeDtypeStruct((6, 2 * nz, 2 * nz), BF),
            jax.ShapeDtypeStruct((6, GROUP * ny, 3 * GROUP * ny), BF),
            jax.ShapeDtypeStruct((6, 2 * nz, 2 * nz), BF),
            jax.ShapeDtypeStruct((6, GROUP * ny // 2, 3 * GROUP * ny), BF),
        ),
        in_specs=[smem] * 3 + [anyw],
        out_specs=[anyw] * 2 + [vmem] * 4,
        scratch_shapes=[pltpu.SemaphoreType.DMA((2, CHUNKS))] * 4,
        compiler_params=pltpu.CompilerParams(
            collective_id=0, has_side_effects=True, vmem_limit_bytes=16 << 20
        ),
        name="exchange",
    )(even_taps, odd_taps, low_taps, density)
    return pl.pallas_call(
        functools.partial(kernel, rows),
        out_shape=jax.ShapeDtypeStruct((per_dev, rows // 2, ny // 2, nz // 2), jnp.float32),
        in_specs=[smem] * 5 + [anyw] * 3 + [vmem] * 4,
        out_specs=vmem,
        scratch_shapes=[
            pltpu.VMEM((rows + 2 * HALO, ny, nz), jnp.float32),
            pltpu.VMEM((NFIRST, rows + 2 * REACH2, ny, nz), jnp.float32),
            pltpu.SemaphoreType.DMA((3,)),
        ],
        compiler_params=pltpu.CompilerParams(vmem_limit_bytes=24 << 20),
        name="scatter",
    )(wavelets, pairs, even_taps, odd_taps, low_taps, before, density, after, z1, y1, z2, y2)


def solution(mesh):
    placed = (P(("groups", "space"), None, None), P(), P(), P(), P(), P())
    return jax.shard_map(
        shards,
        mesh=mesh,
        in_specs=placed,
        out_specs=P("wave", ("groups", "space"), None, None),
        check_vma=False,
    )
```

```python
import functools

import jax
import jax.numpy as jnp
from jax import lax
from jax.experimental import pallas as pl
from jax.experimental.pallas import tpu as pltpu
from jax.sharding import PartitionSpec as P

NFIRST = 5
REACH1 = 14
REACH2 = 28
HALO = REACH1 + REACH2
GROUP = 8
CHUNKS = 3
BF = jnp.bfloat16


def halves(v):
    hi = v.astype(BF)
    return hi, (v - hi.astype(jnp.float32)).astype(BF)


def band(diff, tap_sets, dilation, extent):
    count = tap_sets[0].shape[0]
    totals = [jnp.zeros(diff.shape, jnp.float32) for _ in tap_sets]
    for t in range(count):
        offset = (t - count // 2) * dilation
        if abs(offset) < extent:
            hit = diff == offset
            totals = [jnp.where(hit, s[t], v) for s, v in zip(tap_sets, totals)]
    return totals


def build_tables(filters, ny, nz, z1, y1, z2, y2):
    even, odd, low = filters
    blk = 32

    def iotas(r0, shape):
        r = lax.broadcasted_iota(jnp.int32, shape, 0) + r0
        return r, lax.broadcasted_iota(jnp.int32, shape, 1)

    def put_z(ref, n, r0, value):
        hi, lo = halves(value)
        ref[n, pl.ds(r0, blk), pl.ds(0, nz)] = hi
        ref[n, pl.ds(r0, blk), pl.ds(nz, nz)] = lo
        ref[n, pl.ds(nz + r0, blk), pl.ds(0, nz)] = hi
        ref[n, pl.ds(nz + r0, blk), pl.ds(nz, nz)] = jnp.zeros_like(lo)

    def put_y(ref, n, r0, value):
        hi, lo = halves(value)
        width = GROUP * ny
        ref[n, pl.ds(r0, blk), pl.ds(0, width)] = hi
        ref[n, pl.ds(r0, blk), pl.ds(width, width)] = hi
        ref[n, pl.ds(r0, blk), pl.ds(2 * width, width)] = lo

    for level in (0, 1):
        for r0 in range(0, nz, blk):
            i, j = iotas(r0, (blk, nz))
            for n, v in enumerate(band(i - j, filters, 1 << level, nz)):
                put_z(z1, level * 3 + n, r0, v)
    for stride, ref, levels in ((1, y1, (0, 1)), (2, y2, (1, 2))):
        n_out = ny // stride
        for r0 in range(0, GROUP * n_out, blk):
            r, c = iotas(r0, (blk, GROUP * ny))
            diff = jnp.where(r // n_out == c // ny, c % ny - (r % n_out) * stride, 4 * ny)
            for at, level in enumerate(levels):
                for n, v in enumerate(band(diff, filters, 1 << level, ny)):
                    put_y(ref, at * 3 + n, r0, v)
    half = nz // 2
    for at, level in enumerate((1, 2)):
        for r0 in range(0, nz, blk):
            i, j = iotas(r0, (blk, nz))
            left = j < half
            diff = i - 2 * jnp.where(left, j, j - half)
            e, o, l = band(diff, filters, 1 << level, nz)
            put_z(z2, at * 3, r0, jnp.where(left, l, 0.0))
            put_z(z2, at * 3 + 1, r0, jnp.where(left, 0.0, l))
            put_z(z2, at * 3 + 2, r0, jnp.where(left, e, o))


def exchange(even, odd, low, density, before, after, z1, y1, z2, y2, zsend, zrecv, psend, precv):
    rows, ny, nz = density.shape
    chunk = HALO // 2 // CHUNKS
    count = lax.axis_size("space")
    space = lax.axis_index("space")
    wave = lax.axis_index("wave")
    core = lax.rem(wave, 2)
    partner = wave + 1 - 2 * core
    above = space < count - 1
    below = space > 0
    mesh_ids = pl.DeviceIdType.MESH
    barrier = pltpu.get_barrier_semaphore()

    @pl.when(above)
    def _():
        pl.semaphore_signal(barrier, 1, device_id={"space": space + 1}, device_id_type=mesh_ids)

    @pl.when(below)
    def _():
        pl.semaphore_signal(barrier, 1, device_id={"space": space - 1}, device_id_type=mesh_ids)

    pl.semaphore_signal(barrier, 1, device_id={"wave": partner}, device_id_type=mesh_ids)
    peers = 1 + above.astype(jnp.int32) + below.astype(jnp.int32)
    pl.semaphore_wait(barrier, peers)

    landing = (before, after)
    sends = (above, below)
    arrives = (below, above)

    def zcopy(way, q):
        r = core * (HALO // 2) + q * chunk
        return pltpu.make_async_remote_copy(
            src_ref=density.at[pl.ds(r + (rows - HALO if way == 0 else 0), chunk)],
            dst_ref=landing[way].at[pl.ds(r, chunk)],
            send_sem=zsend.at[way, q],
            recv_sem=zrecv.at[way, q],
            device_id={"space": space + 1 if way == 0 else space - 1},
            device_id_type=mesh_ids,
        )

    def pcopy(way, q, first):
        part = landing[way].at[pl.ds(first * (HALO // 2) + q * chunk, chunk)]
        return pltpu.make_async_remote_copy(
            src_ref=part,
            dst_ref=part,
            send_sem=psend.at[way, q],
            recv_sem=precv.at[way, q],
            device_id={"wave": partner},
            device_id_type=mesh_ids,
        )

    every = [(way, q) for q in range(CHUNKS) for way in range(2)]
    for way, q in every:

        @pl.when(sends[way])
        def _():
            zcopy(way, q).start()

    build_tables((even, odd, low), ny, nz, z1, y1, z2, y2)
    for way, q in every:

        @pl.when(arrives[way])
        def _():
            zcopy(way, q).wait_recv()
            pcopy(way, q, core).start()

    for way, q in every:

        @pl.when(sends[way])
        def _():
            zcopy(way, q).wait_send()

        @pl.when(arrives[way])
        def _():
            pcopy(way, q, core).wait_send()
            pcopy(way, q, 1 - core).wait_recv()


def stacked(v):
    hi, lo = halves(v)
    return jnp.concatenate([hi, lo, hi], axis=0)


def beside(v):
    hi, lo = halves(v)
    return jnp.concatenate([hi, lo], axis=1)


def dot(a, b):
    return jnp.dot(a, b, preferred_element_type=jnp.float32)


def folded(r):
    n = r.shape[1] // 2
    return r[:, :n] + r[:, n:]


def xpass(load, tap_sets):
    count = tap_sets[0].shape[0]
    accs = [[None] * GROUP for _ in tap_sets]
    for t in range(count):
        weights = [s[t] for s in tap_sets]
        for k in range(GROUP):
            plane = load(t, k)
            for n, w in enumerate(weights):
                term = w * plane
                accs[n][k] = term if t == 0 else accs[n][k] + term
    return [jnp.concatenate(a, axis=0) for a in accs]


def ypass(table, tab, xs, orient):
    if orient == 1:
        n, width = table.shape[1:]
        r = dot(table[pl.ds(tab, 2)].reshape(2 * n, width), stacked(xs[0]))
        return [r[:n], r[n:]]
    nz = xs[0].shape[1]
    r = dot(table[tab + 2], jnp.concatenate([stacked(x) for x in xs], axis=1))
    return [r[:, k * nz : (k + 1) * nz] for k in range(len(xs))]


def kernel(
    rows,
    wav,
    pairs,
    even,
    odd,
    low,
    before,
    centre,
    after,
    z1,
    y1,
    z2,
    y2,
    out,
    ext,
    firsts,
    sems,
):
    ny, nz = ext.shape[1], ext.shape[2]
    per_dev = out.shape[0]
    taps_half = even.shape[0] // 2
    fields = rows + 2 * REACH2
    space = lax.axis_index("space")
    last = lax.axis_size("space") - 1
    inner = pltpu.make_async_copy(centre, ext.at[pl.ds(HALO, rows)], sems.at[1])
    inner.start()
    edges = (
        (space > 0, pltpu.make_async_copy(before, ext.at[pl.ds(0, HALO)], sems.at[0]), 0),
        (
            space < last,
            pltpu.make_async_copy(after, ext.at[pl.ds(HALO + rows, HALO)], sems.at[2]),
            HALO + rows,
        ),
    )
    for there, copy, at in edges:

        @pl.when(there)
        def _():
            copy.start()

        @pl.when(jnp.logical_not(there))
        def _():
            ext[pl.ds(at, HALO)] = jnp.zeros((HALO, ny, nz), jnp.float32)

    for there, copy, _ in edges:

        @pl.when(there)
        def _():
            copy.wait()

    inner.wait()
    start = lax.axis_index("wave") * per_dev

    def first_steps(f, orient, unroll):
        level = wav[0, f]
        d = jnp.left_shift(jnp.int32(1), level)
        tab = level * 3

        def step(i, carry):
            chains = []
            for u in range(unroll):
                base = (i * unroll + u) * GROUP + REACH1

                def load(t, k):
                    return ext[base + k + (t - taps_half) * d]

                xs = xpass(load, (even, odd) if orient == 0 else (low,))
                ys = ypass(y1, tab, xs, orient)
                chains.append(ys)
            cols = [beside(jnp.concatenate(c, axis=0)) for c in zip(*chains)]
            if orient == 2:
                re = folded(dot(cols[0], z1[tab]))
                im = folded(dot(cols[0], z1[tab + 1]))
            else:
                re = folded(dot(cols[0], z1[tab + 2]))
                im = folded(dot(cols[1], z1[tab + 2]))
            mag = jnp.sqrt(re * re + im * im + 1e-06)
            planes = unroll * GROUP
            firsts[f, pl.ds(i * planes, planes)] = mag.reshape(planes, ny, nz)
            return carry

        lax.fori_loop(0, fields // (unroll * GROUP), step, 0)

    def do_first(f, carry):
        need = jnp.int32(0)
        for p in range(per_dev):
            need = need + (pairs[0, start + p] == f).astype(jnp.int32)
        for orient in range(3):

            @pl.when((need > 0) & (wav[1, f] == orient))
            def _():
                first_steps(f, orient, 3 if fields % (3 * GROUP) == 0 else 1)

        @pl.when(space == 0)
        def _():
            firsts[f, pl.ds(0, REACH2)] = jnp.zeros((REACH2, ny, nz), jnp.float32)

        @pl.when(space == last)
        def _():
            firsts[f, pl.ds(REACH2 + rows, REACH2)] = jnp.zeros((REACH2, ny, nz), jnp.float32)

        return carry

    lax.fori_loop(0, NFIRST, do_first, 0)

    def second_steps(p, f, w, orient):
        level = wav[0, w]
        d = jnp.left_shift(jnp.int32(1), level)
        tab = (level - 1) * 3
        chains = []
        for g in range(rows // 2 // GROUP):

            def load(t, k):
                return firsts[f, REACH2 + 2 * (g * GROUP + k) + (t - taps_half) * d]

            xs = xpass(load, (even, odd) if orient == 0 else (low,))
            ys = ypass(y2, tab, xs, orient)
            chains.append(ys)
        cols = [beside(jnp.concatenate(c, axis=0)) for c in zip(*chains)]
        if orient == 2:
            r = dot(cols[0], z2[tab + 2])
        else:
            r = dot(cols[0], z2[tab]) + dot(cols[1], z2[tab + 1])
        v = folded(r)
        sq = v * v
        total = sq + pltpu.roll(sq, nz // 2, 1)
        mag = jnp.sqrt(total + 1e-06)[:, : nz // 2]
        out[p] = mag.reshape(out.shape[1:])

    def do_pair(p, carry):
        f = pairs[0, start + p]
        w = pairs[1, start + p]
        for orient in range(3):

            @pl.when((f >= 0) & (wav[1, w] == orient))
            def _():
                second_steps(p, f, w, orient)

        @pl.when(f < 0)
        def _():
            out[p] = jnp.zeros(out.shape[1:], jnp.float32)

        return carry

    lax.fori_loop(0, per_dev, do_pair, 0)


def shards(density, even_taps, odd_taps, low_taps, wavelets, pairs):
    rows, ny, nz = density.shape
    per_dev = pairs.shape[0] // lax.axis_size("wave")
    smem = pl.BlockSpec(memory_space=pltpu.SMEM)
    vmem = pl.BlockSpec(memory_space=pltpu.VMEM)
    anyw = pl.BlockSpec(memory_space=pl.ANY)
    hbm = pl.BlockSpec(memory_space=pltpu.HBM)
    halo = jax.ShapeDtypeStruct((HALO, ny, nz), jnp.float32)
    before, after, z1, y1, z2, y2 = pl.pallas_call(
        exchange,
        out_shape=(
            halo,
            halo,
            jax.ShapeDtypeStruct((6, 2 * nz, 2 * nz), BF),
            jax.ShapeDtypeStruct((6, GROUP * ny, 3 * GROUP * ny), BF),
            jax.ShapeDtypeStruct((6, 2 * nz, 2 * nz), BF),
            jax.ShapeDtypeStruct((6, GROUP * ny // 2, 3 * GROUP * ny), BF),
        ),
        in_specs=[smem] * 3 + [hbm],
        out_specs=[anyw] * 2 + [vmem] * 4,
        scratch_shapes=[pltpu.SemaphoreType.DMA((2, CHUNKS))] * 4,
        compiler_params=pltpu.CompilerParams(
            collective_id=0, has_side_effects=True, vmem_limit_bytes=16 << 20
        ),
        name="exchange",
    )(even_taps, odd_taps, low_taps, density)
    return pl.pallas_call(
        functools.partial(kernel, rows),
        out_shape=jax.ShapeDtypeStruct((per_dev, rows // 2, ny // 2, nz // 2), jnp.float32),
        in_specs=[smem] * 5 + [anyw, hbm, anyw] + [vmem] * 4,
        out_specs=vmem,
        scratch_shapes=[
            pltpu.VMEM((rows + 2 * HALO, ny, nz), jnp.float32),
            pltpu.VMEM((NFIRST, rows + 2 * REACH2, ny, nz), jnp.float32),
            pltpu.SemaphoreType.DMA((3,)),
        ],
        compiler_params=pltpu.CompilerParams(vmem_limit_bytes=24 << 20),
        name="scatter",
    )(wavelets.T, pairs.T, even_taps, odd_taps, low_taps, before, density, after, z1, y1, z2, y2)


def solution(mesh):
    placed = (P(("groups", "space"), None, None), P(), P(), P(), P(), P())
    return jax.shard_map(
        shards,
        mesh=mesh,
        in_specs=placed,
        out_specs=P("wave", ("groups", "space"), None, None),
        check_vma=False,
    )
```

```python
import functools

import jax
import jax.numpy as jnp
from jax import lax
from jax.experimental import pallas as pl
from jax.experimental.pallas import tpu as pltpu
from jax.sharding import PartitionSpec as P

NFIRST = 5
REACH1 = 14
REACH2 = 28
HALO = REACH1 + REACH2
GROUP = 8
CHUNKS = 3
BF = jnp.bfloat16


def halves(v):
    hi = v.astype(BF)
    return hi, (v - hi.astype(jnp.float32)).astype(BF)


def band(diff, tap_sets, dilation, extent):
    count = tap_sets[0].shape[0]
    totals = [jnp.zeros(diff.shape, jnp.float32) for _ in tap_sets]
    for t in range(count):
        offset = (t - count // 2) * dilation
        if abs(offset) < extent:
            hit = diff == offset
            totals = [jnp.where(hit, s[t], v) for s, v in zip(tap_sets, totals)]
    return totals


def build_tables(filters, ny, nz, z1, y1, z2, y2):
    even, odd, low = filters
    blk = 32

    def iotas(r0, shape):
        r = lax.broadcasted_iota(jnp.int32, shape, 0) + r0
        return r, lax.broadcasted_iota(jnp.int32, shape, 1)

    def put_z(ref, n, r0, value):
        hi, lo = halves(value)
        ref[n, pl.ds(r0, blk), pl.ds(0, nz)] = hi
        ref[n, pl.ds(r0, blk), pl.ds(nz, nz)] = lo
        ref[n, pl.ds(nz + r0, blk), pl.ds(0, nz)] = hi
        ref[n, pl.ds(nz + r0, blk), pl.ds(nz, nz)] = jnp.zeros_like(lo)

    def put_y(ref, n, r0, value):
        hi, lo = halves(value)
        width = GROUP * ny
        ref[n, pl.ds(r0, blk), pl.ds(0, width)] = hi
        ref[n, pl.ds(r0, blk), pl.ds(width, width)] = hi
        ref[n, pl.ds(r0, blk), pl.ds(2 * width, width)] = lo

    for level in (0, 1):
        for r0 in range(0, nz, blk):
            i, j = iotas(r0, (blk, nz))
            for n, v in enumerate(band(i - j, filters, 1 << level, nz)):
                put_z(z1, level * 3 + n, r0, v)
    for stride, ref, levels in ((1, y1, (0, 1)), (2, y2, (1, 2))):
        n_out = ny // stride
        for r0 in range(0, GROUP * n_out, blk):
            r, c = iotas(r0, (blk, GROUP * ny))
            diff = jnp.where(r // n_out == c // ny, c % ny - (r % n_out) * stride, 4 * ny)
            for at, level in enumerate(levels):
                for n, v in enumerate(band(diff, filters, 1 << level, ny)):
                    put_y(ref, at * 3 + n, r0, v)
    half = nz // 2
    for at, level in enumerate((1, 2)):
        for r0 in range(0, nz, blk):
            i, j = iotas(r0, (blk, nz))
            left = j < half
            diff = i - 2 * jnp.where(left, j, j - half)
            e, o, l = band(diff, filters, 1 << level, nz)
            put_z(z2, at * 3, r0, jnp.where(left, l, 0.0))
            put_z(z2, at * 3 + 1, r0, jnp.where(left, 0.0, l))
            put_z(z2, at * 3 + 2, r0, jnp.where(left, e, o))


def exchange(wav, pairs, even, odd, low, density, before, after, z1, y1, z2, y2, zsend, zrecv, psend, precv):
    rows, ny, nz = density.shape
    chunk = HALO // 2 // CHUNKS
    count = lax.axis_size("space")
    space = lax.axis_index("space")
    wave = lax.axis_index("wave")
    core = lax.rem(wave, 2)
    partner = wave + 1 - 2 * core
    above = space < count - 1
    below = space > 0
    mesh_ids = pl.DeviceIdType.MESH
    barrier = pltpu.get_barrier_semaphore()

    @pl.when(above)
    def _():
        pl.semaphore_signal(barrier, 1, device_id={"space": space + 1}, device_id_type=mesh_ids)

    @pl.when(below)
    def _():
        pl.semaphore_signal(barrier, 1, device_id={"space": space - 1}, device_id_type=mesh_ids)

    pl.semaphore_signal(barrier, 1, device_id={"wave": partner}, device_id_type=mesh_ids)
    peers = 1 + above.astype(jnp.int32) + below.astype(jnp.int32)
    pl.semaphore_wait(barrier, peers)

    landing = (before, after)
    sends = (above, below)
    arrives = (below, above)

    def zcopy(way, q):
        r = core * (HALO // 2) + q * chunk
        return pltpu.make_async_remote_copy(
            src_ref=density.at[pl.ds(r + (rows - HALO if way == 0 else 0), chunk)],
            dst_ref=landing[way].at[pl.ds(r, chunk)],
            send_sem=zsend.at[way, q],
            recv_sem=zrecv.at[way, q],
            device_id={"space": space + 1 if way == 0 else space - 1},
            device_id_type=mesh_ids,
        )

    def pcopy(way, q, first):
        part = landing[way].at[pl.ds(first * (HALO // 2) + q * chunk, chunk)]
        return pltpu.make_async_remote_copy(
            src_ref=part,
            dst_ref=part,
            send_sem=psend.at[way, q],
            recv_sem=precv.at[way, q],
            device_id={"wave": partner},
            device_id_type=mesh_ids,
        )

    every = [(way, q) for q in range(CHUNKS) for way in range(2)]
    for way, q in every:

        @pl.when(sends[way])
        def _():
            zcopy(way, q).start()

    build_tables((even, odd, low), ny, nz, z1, y1, z2, y2)
    for way, q in every:

        @pl.when(arrives[way])
        def _():
            zcopy(way, q).wait_recv()
            pcopy(way, q, core).start()

    for way, q in every:

        @pl.when(sends[way])
        def _():
            zcopy(way, q).wait_send()

        @pl.when(arrives[way])
        def _():
            pcopy(way, q, core).wait_send()
            pcopy(way, q, 1 - core).wait_recv()


def stacked(v):
    hi, lo = halves(v)
    return jnp.concatenate([hi, lo, hi], axis=0)


def beside(v):
    hi, lo = halves(v)
    return jnp.concatenate([hi, lo], axis=1)


def dot(a, b):
    return jnp.dot(a, b, preferred_element_type=jnp.float32)


def folded(r):
    n = r.shape[1] // 2
    return r[:, :n] + r[:, n:]


def xpass(load, tap_sets):
    count = tap_sets[0].shape[0]
    accs = [[None] * GROUP for _ in tap_sets]
    for t in range(count):
        weights = [s[t] for s in tap_sets]
        for k in range(GROUP):
            plane = load(t, k)
            for n, w in enumerate(weights):
                term = w * plane
                accs[n][k] = term if t == 0 else accs[n][k] + term
    return [jnp.concatenate(a, axis=0) for a in accs]


def ypass(table, tab, xs, orient):
    if orient == 1:
        n, width = table.shape[1:]
        r = dot(table[pl.ds(tab, 2)].reshape(2 * n, width), stacked(xs[0]))
        return [r[:n], r[n:]]
    nz = xs[0].shape[1]
    r = dot(table[tab + 2], jnp.concatenate([stacked(x) for x in xs], axis=1))
    return [r[:, k * nz : (k + 1) * nz] for k in range(len(xs))]


def kernel(
    rows,
    wav,
    pairs,
    even,
    odd,
    low,
    before,
    centre,
    after,
    z1,
    y1,
    z2,
    y2,
    out,
    ext,
    firsts,
    sems,
):
    ny, nz = ext.shape[1], ext.shape[2]
    per_dev = out.shape[0]
    taps_half = even.shape[0] // 2
    fields = rows + 2 * REACH2
    space = lax.axis_index("space")
    last = lax.axis_size("space") - 1
    inner = pltpu.make_async_copy(centre, ext.at[pl.ds(HALO, rows)], sems.at[1])
    inner.start()
    edges = (
        (space > 0, pltpu.make_async_copy(before, ext.at[pl.ds(0, HALO)], sems.at[0]), 0),
        (
            space < last,
            pltpu.make_async_copy(after, ext.at[pl.ds(HALO + rows, HALO)], sems.at[2]),
            HALO + rows,
        ),
    )
    for there, copy, at in edges:

        @pl.when(there)
        def _():
            copy.start()

        @pl.when(jnp.logical_not(there))
        def _():
            ext[pl.ds(at, HALO)] = jnp.zeros((HALO, ny, nz), jnp.float32)

    for there, copy, _ in edges:

        @pl.when(there)
        def _():
            copy.wait()

    inner.wait()
    start = lax.axis_index("wave") * per_dev

    def first_steps(f, orient, unroll):
        level = wav[0, f]
        d = jnp.left_shift(jnp.int32(1), level)
        tab = level * 3

        def step(i, carry):
            chains = []
            for u in range(unroll):
                base = (i * unroll + u) * GROUP + REACH1

                def load(t, k):
                    return ext[base + k + (t - taps_half) * d]

                xs = xpass(load, (even, odd) if orient == 0 else (low,))
                ys = ypass(y1, tab, xs, orient)
                chains.append(ys)
            cols = [beside(jnp.concatenate(c, axis=0)) for c in zip(*chains)]
            if orient == 2:
                re = folded(dot(cols[0], z1[tab]))
                im = folded(dot(cols[0], z1[tab + 1]))
            else:
                re = folded(dot(cols[0], z1[tab + 2]))
                im = folded(dot(cols[1], z1[tab + 2]))
            mag = jnp.sqrt(re * re + im * im + 1e-06)
            planes = unroll * GROUP
            firsts[f, pl.ds(i * planes, planes)] = mag.reshape(planes, ny, nz)
            return carry

        lax.fori_loop(0, fields // (unroll * GROUP), step, 0)

    def do_first(f, carry):
        need = jnp.int32(0)
        for p in range(per_dev):
            need = need + (pairs[0, start + p] == f).astype(jnp.int32)
        for orient in range(3):

            @pl.when((need > 0) & (wav[1, f] == orient))
            def _():
                first_steps(f, orient, 3 if fields % (3 * GROUP) == 0 else 1)

        @pl.when(space == 0)
        def _():
            firsts[f, pl.ds(0, REACH2)] = jnp.zeros((REACH2, ny, nz), jnp.float32)

        @pl.when(space == last)
        def _():
            firsts[f, pl.ds(REACH2 + rows, REACH2)] = jnp.zeros((REACH2, ny, nz), jnp.float32)

        return carry

    lax.fori_loop(0, NFIRST, do_first, 0)

    def second_steps(p, f, w, orient):
        level = wav[0, w]
        d = jnp.left_shift(jnp.int32(1), level)
        tab = (level - 1) * 3
        chains = []
        for g in range(rows // 2 // GROUP):

            def load(t, k):
                return firsts[f, REACH2 + 2 * (g * GROUP + k) + (t - taps_half) * d]

            xs = xpass(load, (even, odd) if orient == 0 else (low,))
            ys = ypass(y2, tab, xs, orient)
            chains.append(ys)
        cols = [beside(jnp.concatenate(c, axis=0)) for c in zip(*chains)]
        if orient == 2:
            r = dot(cols[0], z2[tab + 2])
        else:
            r = dot(cols[0], z2[tab]) + dot(cols[1], z2[tab + 1])
        v = folded(r)
        sq = v * v
        total = sq + pltpu.roll(sq, nz // 2, 1)
        mag = jnp.sqrt(total + 1e-06)[:, : nz // 2]
        out[p] = mag.reshape(out.shape[1:])

    def do_pair(p, carry):
        f = pairs[0, start + p]
        w = pairs[1, start + p]
        for orient in range(3):

            @pl.when((f >= 0) & (wav[1, w] == orient))
            def _():
                second_steps(p, f, w, orient)

        @pl.when(f < 0)
        def _():
            out[p] = jnp.zeros(out.shape[1:], jnp.float32)

        return carry

    lax.fori_loop(0, per_dev, do_pair, 0)


def shards(density, even_taps, odd_taps, low_taps, wavelets, pairs):
    rows, ny, nz = density.shape
    per_dev = pairs.shape[0] // lax.axis_size("wave")
    smem = pl.BlockSpec(memory_space=pltpu.SMEM)
    vmem = pl.BlockSpec(memory_space=pltpu.VMEM)
    anyw = pl.BlockSpec(memory_space=pl.ANY)
    hbm = pl.BlockSpec(memory_space=pltpu.HBM)
    density = pltpu.with_memory_space_constraint(density, pltpu.HBM)
    halo = jax.ShapeDtypeStruct((HALO, ny, nz), jnp.float32)
    before, after, z1, y1, z2, y2 = pl.pallas_call(
        exchange,
        out_shape=(
            halo,
            halo,
            jax.ShapeDtypeStruct((6, 2 * nz, 2 * nz), BF),
            jax.ShapeDtypeStruct((6, GROUP * ny, 3 * GROUP * ny), BF),
            jax.ShapeDtypeStruct((6, 2 * nz, 2 * nz), BF),
            jax.ShapeDtypeStruct((6, GROUP * ny // 2, 3 * GROUP * ny), BF),
        ),
        in_specs=[smem] * 5 + [hbm],
        out_specs=[anyw] * 2 + [vmem] * 4,
        scratch_shapes=[pltpu.SemaphoreType.DMA((2, CHUNKS))] * 4,
        compiler_params=pltpu.CompilerParams(
            collective_id=0, has_side_effects=True, vmem_limit_bytes=16 << 20
        ),
        name="exchange",
    )(wavelets.T, pairs.T, even_taps, odd_taps, low_taps, density)
    return pl.pallas_call(
        functools.partial(kernel, rows),
        out_shape=jax.ShapeDtypeStruct((per_dev, rows // 2, ny // 2, nz // 2), jnp.float32),
        in_specs=[smem] * 5 + [anyw, hbm, anyw] + [vmem] * 4,
        out_specs=vmem,
        scratch_shapes=[
            pltpu.VMEM((rows + 2 * HALO, ny, nz), jnp.float32),
            pltpu.VMEM((NFIRST, rows + 2 * REACH2, ny, nz), jnp.float32),
            pltpu.SemaphoreType.DMA((3,)),
        ],
        compiler_params=pltpu.CompilerParams(vmem_limit_bytes=24 << 20),
        name="scatter",
    )(wavelets.T, pairs.T, even_taps, odd_taps, low_taps, before, density, after, z1, y1, z2, y2)


def solution(mesh):
    placed = (P(("groups", "space"), None, None), P(), P(), P(), P(), P())
    return jax.shard_map(
        shards,
        mesh=mesh,
        in_specs=placed,
        out_specs=P("wave", ("groups", "space"), None, None),
        check_vma=False,
    )
```
